32 devices in a mesh: survey: 2 (over x), chan: 16 (over z, y, core).
Axes of the slice: x: 2, y: 2, z: 4, core: 2. Of those that a mesh axis runs over, the one named last changes fastest.
Arguments:
- das_window: float32 [8192, 8192], P(('survey', 'chan')), parts along dimension 0, may hold values from -6 to 6
- fan_bound: int32 [4096], replicated, may hold values from -1 to 2048, as said below
- tap_offset: int32 [8, 32], replicated, may hold values from -31 to 31, as said below
- tap_weight: float32 [8, 32], replicated, may hold values from -1 to 1
Outputs:
- filtered: float32 [8192, 8192], P(('survey', 'chan')), parts along dimension 0
- energy: float32 [8192, 8, 128], P(('survey', 'chan')), parts along dimension 0
The draws below stay inside these ranges and needn't reach their ends.
There are 2 independent parts, one for each index of `survey`. The reference program is written for one: setup_inputs(seed, part) draws one part's arguments, and reference() takes and returns one part's arrays. A program takes and returns all parts, laid end to end along the dimension named above; an argument that names none is the same for every part. Nothing has to cross between parts.
Inputs may be any that keep to these rules, and one draw needn't show every extreme that they name: `fan_bound`: entry f bounds the magnitude of the signed channel wavenumber bin passed at the time frequency bins +f and -f; -1 passes none. `tap_offset`: the channel offset of a tap relative to the output channel.
All inputs are finite; a program needn't handle non-finite values.
Results may differ from the reference program's by a relative error of at most 0.0027.
Values may be sent and summed in bfloat16 or wider, within the bound.
No kernel may reach another device: no remote copies, remote signals or barrier semaphores. Data moves between devices by JAX's collectives and lax.ppermute only.
A program may use at most 256 MiB of HBM per device.

```python
import jax
import jax.numpy as jnp
from jax import lax

S = 8192
HALO = 31
TEMPLATES = 8
TAPS = 32
WIN = 64
C = 4096


def draw_fan_bound(key, part):
    freq_index = jnp.arange(S // 2, dtype=jnp.int32)
    low_cut = jax.random.randint(jax.random.fold_in(key, 1), (), 1, max(2, S // 8))
    slope_rate = jax.random.randint(jax.random.fold_in(key, 2), (), 3, 7)
    jitter_span = max(1, C // 256)
    jitter = jax.random.randint(jax.random.fold_in(key, 3), (S // 2,), -jitter_span, jitter_span + 1)
    linear = (freq_index - low_cut) * slope_rate * C // (2 * S)
    bounded = jnp.clip(linear + jitter, -1, C // 2)
    bounded = jnp.where(freq_index < low_cut, -1, bounded)
    return bounded.astype(jnp.int32)


def draw_tap_offset(key, part):
    raw_offsets = jax.random.randint(jax.random.fold_in(key, 1), (TEMPLATES * TAPS,), -HALO, HALO + 1)
    ordering = jax.random.permutation(jax.random.fold_in(key, 2), TEMPLATES * TAPS)
    raw_offsets = raw_offsets.at[ordering[0]].set(-HALO)
    raw_offsets = raw_offsets.at[ordering[1]].set(HALO)
    return raw_offsets.reshape(TEMPLATES, TAPS).astype(jnp.int32)


def block_scale(key, shape, cuts, smallest, largest):
    loudness = 1.0
    for position, blocks in cuts:
        draws = jax.random.uniform(jax.random.fold_in(jax.random.fold_in(key, 6), position), (blocks,), jnp.float32, smallest / len(cuts), largest / len(cuts))
        loudness = loudness * jnp.repeat(jnp.exp(draws), shape[position] // blocks).reshape((-1,) + (1,) * (len(shape) - 1 - position))
    return loudness


def noise(stream_key, dims, width, most, split=(), kind=jnp.bfloat16):
    values = jax.random.normal(stream_key, dims, jnp.float32) * width
    if len(split) > 0:
        values = block_scale(stream_key, dims, split, -0.22, 0.18) * values
    return jnp.clip(values, min=-most, max=most).astype(kind)


def setup_inputs(seed: int = 0, part: int = 0) -> dict:
    keys = jax.random.split(jax.random.key(seed), 5)
    part_keys = jax.random.split(jax.random.fold_in(keys[4], part), 5)
    return {
        "das_window": noise(part_keys[0], (C, S), 1.0, 6.0, ((0, 16),), jnp.float32),
        "fan_bound": draw_fan_bound(jax.random.fold_in(keys[4], 71), part),
        "tap_offset": draw_tap_offset(jax.random.fold_in(keys[4], 71), part),
        "tap_weight": noise(keys[3], (TEMPLATES, TAPS), TAPS ** -0.5, 1.0, (), jnp.float32),
    }


def reference(das_window, fan_bound, tap_offset, tap_weight):
    spectrum = jnp.fft.fft2(das_window)
    chan_index = jnp.arange(C, dtype=jnp.int32)
    chan_signed = jnp.where(chan_index < C // 2, chan_index, chan_index - C)
    time_index = jnp.arange(S, dtype=jnp.int32)
    time_signed = jnp.where(time_index < S // 2, time_index, time_index - S)
    extended = jnp.concatenate([fan_bound, jnp.full((1,), -1, jnp.int32)])
    limits = jnp.take(extended, jnp.abs(time_signed).astype(jnp.int32))
    passing = jnp.abs(chan_signed)[:, None] <= limits[None, :]
    filtered = jnp.fft.ifft2(jnp.where(passing, spectrum, 0.0)).real.astype(jnp.float32)
    rounded = filtered.astype(jnp.bfloat16)
    low_field = lax.optimization_barrier(rounded).astype(jnp.float32)
    offsets_grid = jnp.arange(2 * HALO + 1, dtype=jnp.int32) - HALO
    matches = (tap_offset[:, :, None] == offsets_grid[None, None, :]).astype(jnp.float32)
    kernel_low = jnp.sum(tap_weight[:, :, None] * matches, axis=1).astype(jnp.bfloat16)
    kernel_wide = lax.optimization_barrier(kernel_low).astype(jnp.float32)
    padded = jnp.pad(low_field, ((HALO, HALO), (0, 0)))

    def one_template(weights):
        def add_offset(offset, running):
            return running + weights[offset] * lax.dynamic_slice_in_dim(padded, offset, C, 0)

        detection = lax.fori_loop(0, 2 * HALO + 1, add_offset, jnp.zeros((C, S), jnp.float32))
        return jnp.mean((detection * detection).reshape(C, S // WIN, WIN), axis=2)

    energy = lax.map(one_template, kernel_wide)
    return filtered, jnp.transpose(energy, (1, 0, 2))
```

```python
import math
import jax
import jax.numpy as jnp
import numpy as np
from jax import lax
from jax.experimental import pallas as pl
from jax.experimental.pallas import tpu as pltpu
from jax.sharding import PartitionSpec as P

HALO = 31
EDGE = 32
WIN = 64
LANES = 128
BF = jnp.bfloat16
F32 = jnp.float32
VMEM_BYTES = 58 * 1024 * 1024


def cadd(x, y):
    return (x[0] + y[0], x[1] + y[1])


def csub(x, y):
    return (x[0] - y[0], x[1] - y[1])


def cmul_const(x, angle_num, angle_den):
    num = angle_num % angle_den
    if num == 0:
        return x
    if 2 * num == angle_den:
        return (-x[0], -x[1])
    if 4 * num == angle_den:
        return (-x[1], x[0])
    if 4 * num == 3 * angle_den:
        return (x[1], -x[0])
    theta = 2.0 * math.pi * num / angle_den
    c, s = math.cos(theta), math.sin(theta)
    if (8 * num) % angle_den == 0:
        h = math.sqrt(0.5)
        cs, ss = (1 if c > 0 else -1), (1 if s > 0 else -1)
        if cs == ss:
            return ((x[0] - x[1]) * (h * cs), (x[0] + x[1]) * (h * cs))
        return ((x[0] + x[1]) * (h * cs), (x[1] - x[0]) * (h * cs))
    return (x[0] * c - x[1] * s, x[0] * s + x[1] * c)


def cfft(xs, sign):
    n = len(xs)
    if n == 1:
        return list(xs)
    if n == 2:
        return [cadd(xs[0], xs[1]), csub(xs[0], xs[1])]
    u = cfft(xs[0::2], sign)
    z = cfft(xs[1::4], sign)
    zp = cfft(xs[3::4], sign)
    out = [None] * n
    q = n // 4
    for k in range(q):
        a = cmul_const(z[k], sign * k, n)
        b = cmul_const(zp[k], sign * 3 * k, n)
        s = cadd(a, b)
        d = csub(a, b)
        t = (-d[1], d[0]) if sign > 0 else (d[1], -d[0])
        out[k] = cadd(u[k], s)
        out[k + 2 * q] = csub(u[k], s)
        out[k + q] = cadd(u[k + q], t)
        out[k + 3 * q] = csub(u[k + q], t)
    return out


def conj(x):
    return (x[0], -x[1])


def rfft(xs):
    n = len(xs)
    if n == 1:
        return [(xs[0], None)]
    if n == 2:
        return [(xs[0] + xs[1], None), (xs[0] - xs[1], None)]
    u = rfft(xs[0::2])
    z = rfft(xs[1::4])
    zp = rfft(xs[3::4])
    q = n // 4
    out = [None] * (n // 2 + 1)

    def bin_of(v, size, k):
        k = k % size
        if 2 * k <= size:
            return v[k]
        w = v[size - k]
        return w if w[1] is None else (w[0], -w[1])

    for k in range(q // 2 + 1):
        if k == 0:
            s = z[0][0] + zp[0][0]
            d = z[0][0] - zp[0][0]
            out[0] = (u[0][0] + s, None)
            out[2 * q] = (u[0][0] - s, None)
            out[q] = (u[q][0], -d)
            continue
        zk = bin_of(z, q, k)
        zpk = bin_of(zp, q, k)
        if zk[1] is None:
            zc = lambda v, num: (v * math.cos(2 * math.pi * num / n), v * math.sin(2 * math.pi * num / n))
            a = zc(zk[0], -k)
            b = zc(zpk[0], -3 * k)
        else:
            a = cmul_const(zk, -k, n)
            b = cmul_const(zpk, -3 * k, n)
        s = cadd(a, b)
        d = csub(a, b)
        uk = u[k] if u[k][1] is not None else (u[k][0], 0.0)
        uq = bin_of(u, 2 * q, k + q)
        uq = uq if uq[1] is not None else (uq[0], 0.0)
        out[k] = cadd(uk, s)
        out[2 * q - k] = (uk[0] - s[0], s[1] - uk[1])
        if k + q != 2 * q - k:
            out[q + k] = (uq[0] + d[1], uq[1] - d[0])
        if q - k != k:
            out[q - k] = (uq[0] - d[1], -(uq[1] + d[0]))
    return out


def c2r(hs, n):
    if n == 1:
        return [hs[0][0]]
    if n == 2:
        return [hs[0][0] + hs[1][0], hs[0][0] - hs[1][0]]
    half = n // 2
    even, odd = [], []
    for k in range(half // 2 + 1):
        a = hs[k]
        b = hs[half - k]
        if k == 0:
            even.append((a[0] + b[0], None))
            odd.append((a[0] - b[0], None))
        elif 2 * k == half:
            even.append((a[0] + a[0], None))
            odd.append((-(a[1] + a[1]), None))
        else:
            even.append((a[0] + b[0], a[1] - b[1]))
            odd.append(cmul_const((a[0] - b[0], a[1] + b[1]), k, n))
    e = c2r(even, half)
    o = c2r(odd, half)
    out = [None] * n
    out[0::2] = e
    out[1::2] = o
    return out


def split_bf(x):
    hi = x.astype(BF)
    lo = (x - hi.astype(F32)).astype(BF)
    return hi, lo


def mm(a, b):
    return jnp.dot(a, b, preferred_element_type=F32)


def np_split(t):
    t = np.asarray(t, np.float64)
    hi = t.astype(np.float32).astype(BF)
    lo = (t - hi.astype(np.float64)).astype(np.float32).astype(BF)
    return hi, lo


def phase(n, modulus):
    theta = 2.0 * np.pi * (np.asarray(n, np.int64) % modulus) / modulus
    return np.cos(theta), np.sin(theta)


def time_tables(samples, inner):
    outer = samples // inner
    b = np.arange(inner)[:, None]
    m = np.arange(inner // 2)[None, :]
    c, s = phase(b * m, inner)
    fwd = np.block([[c, -s], [s, c]])
    inv = np.block([[c.T, s.T], [-s.T, c.T]])
    k1 = np.arange(outer)[:, None]
    bb = np.arange(inner)[None, :]
    tc, ts = phase(k1 * bb, samples)
    return fwd, inv, tc.astype(np.float32), ts.astype(np.float32)


def chan_tables(channels, inner):
    outer = channels // inner
    q = np.arange(inner)[:, None]
    c0 = np.arange(inner)[None, :]
    c, s = phase(q * c0, inner)
    fwd = np.block([[c, s], [-s, c]])
    inv = np.block([[c.T, -s.T], [s.T, c.T]])
    p = np.arange(outer)[:, None]
    tc, ts = phase(p * np.arange(inner)[None, :], channels)
    return fwd, inv, tc.astype(np.float32), ts.astype(np.float32)


def time_forward(x, th, tl, tc, ts, inner, rows):
    row_count, samples = x.shape
    outer = samples // inner
    half = inner // 2
    tiles = inner // LANES
    sub = 16

    def body(x_ref, th_ref, tl_ref, tc_ref, ts_ref, o_ref, yh_ref, yl_ref):
        def group(g, carry):
            r0 = pl.multiple_of(g * sub, sub)
            for h in range(tiles):
                lanes = slice(h * LANES, (h + 1) * LANES)
                xs = [x_ref[pl.ds(r0, sub), a * inner + h * LANES : a * inner + (h + 1) * LANES] for a in range(outer)]
                ys = rfft(xs)
                for k in range(outer):
                    src = ys[k] if 2 * k <= outer else ys[outer - k]
                    neg = 2 * k > outer
                    c = tc_ref[k : k + 1, lanes]
                    s = ts_ref[k : k + 1, lanes]
                    if src[1] is None:
                        yr, yi = src[0] * c, -(src[0] * s)
                    elif neg:
                        yr = src[0] * c - src[1] * s
                        yi = -(src[0] * s + src[1] * c)
                    else:
                        yr = src[0] * c + src[1] * s
                        yi = src[1] * c - src[0] * s
                    rh, rl = split_bf(yr)
                    ih, il = split_bf(yi)
                    yh_ref[k, pl.ds(r0, sub), lanes] = rh
                    yl_ref[k, pl.ds(r0, sub), lanes] = rl
                    ilanes = slice(inner + h * LANES, inner + (h + 1) * LANES)
                    yh_ref[k, pl.ds(r0, sub), ilanes] = ih
                    yl_ref[k, pl.ds(r0, sub), ilanes] = il
            return carry

        lax.fori_loop(0, rows // sub, group, 0)
        per = 8

        def product(g, carry):
            k0 = pl.multiple_of(g * per, per)
            yh = yh_ref[pl.ds(k0, per)].reshape(per * rows, 2 * inner)
            yl = yl_ref[pl.ds(k0, per)].reshape(per * rows, 2 * inner)
            z = mm(yh, th_ref[...]) + mm(yl, th_ref[...]) + mm(yh, tl_ref[...])
            z = z.astype(BF).reshape(per, rows, 2 * half)
            o_ref[pl.ds(k0, per), 0] = z[:, :, :half]
            o_ref[pl.ds(k0, per), 1] = z[:, :, half:]
            return carry

        lax.fori_loop(0, outer // per, product, 0)

    full = lambda a: pl.BlockSpec(a.shape, lambda i: (0,) * a.ndim)
    return pl.pallas_call(
        body,
        grid=(row_count // rows,),
        in_specs=[pl.BlockSpec((rows, samples), lambda i: (i, 0)), full(th), full(tl), full(tc), full(ts)],
        out_specs=pl.BlockSpec((outer, 2, rows, half), lambda i: (0, 0, i, 0)),
        out_shape=jax.ShapeDtypeStruct((outer, 2, row_count, half), BF),
        scratch_shapes=[pltpu.VMEM((outer, rows, 2 * inner), BF)] * 2,
        compiler_params=pltpu.CompilerParams(vmem_limit_bytes=VMEM_BYTES),
        name="time_forward",
    )(x, th, tl, tc, ts)


def channel_filter(z, limit, weight, fh, fl, gh, gl, tc, ts, inner):
    peers, own, _, row_count, bins = z.shape
    channels = peers * row_count
    outer = channels // inner
    per_peer = row_count // inner
    sub = 16

    def body(z_ref, lim_ref, wt_ref, fh_ref, fl_ref, gh_ref, gl_ref, tc_ref, ts_ref, o_ref, v_ref, w_ref):
        def fwd(g, carry):
            r0 = pl.multiple_of(g * sub, sub)
            xs = []
            for c1 in range(outer):
                peer, part = c1 // per_peer, c1 % per_peer
                rr = pl.ds(part * inner + r0, sub)
                xs.append((z_ref[peer, 0, 0, rr, :].astype(F32), z_ref[peer, 0, 1, rr, :].astype(F32)))
            vs = cfft(xs, -1)
            for p in range(outer):
                c = tc_ref[p, pl.ds(r0, sub), :]
                s = ts_ref[p, pl.ds(r0, sub), :]
                vr, vi = vs[p]
                rh, rl = split_bf(vr * c + vi * s)
                ih, il = split_bf(vi * c - vr * s)
                v_ref[p, pl.ds(r0, sub), :bins] = rh
                v_ref[p, pl.ds(r0, sub), bins:] = rl
                v_ref[p, pl.ds(inner + r0, sub), :bins] = ih
                v_ref[p, pl.ds(inner + r0, sub), bins:] = il
            return carry

        lax.fori_loop(0, inner // sub, fwd, 0)
        limit_row = lim_ref[0]
        weight_row = wt_ref[0]
        q_index = lax.broadcasted_iota(jnp.int32, (inner, bins), 0)

        def middle(p, carry):
            v = v_ref[p]
            u2 = mm(fh_ref[...], v)
            u = u2[:, :bins] + u2[:, bins:] + mm(fl_ref[...], v[:, :bins])
            kc = p + outer * q_index
            kc = jnp.where(kc < channels // 2, kc, channels - kc)
            gain = jnp.where(kc <= limit_row, weight_row, 0.0)
            uh, ul = split_bf(jnp.concatenate([u[:inner] * gain, u[inner:] * gain], axis=0))
            w2 = mm(gh_ref[...], jnp.concatenate([uh, ul], axis=1))
            w = w2[:, :bins] + w2[:, bins:] + mm(gl_ref[...], uh)
            c = tc_ref[p]
            s = ts_ref[p]
            wr, wi = w[:inner], w[inner:]
            w_ref[p, 0] = wr * c - wi * s
            w_ref[p, 1] = wr * s + wi * c
            return carry

        lax.fori_loop(0, outer, middle, 0, unroll=2)

        def back(g, carry):
            r0 = pl.multiple_of(g * sub, sub)
            ws = [(w_ref[p, 0, pl.ds(r0, sub), :], w_ref[p, 1, pl.ds(r0, sub), :]) for p in range(outer)]
            ys = cfft(ws, 1)
            for c1 in range(outer):
                peer, part = c1 // per_peer, c1 % per_peer
                rr = pl.ds(part * inner + r0, sub)
                o_ref[peer, 0, 0, rr, :] = ys[c1][0].astype(BF)
                o_ref[peer, 0, 1, rr, :] = ys[c1][1].astype(BF)
            return carry

        lax.fori_loop(0, inner // sub, back, 0)

    full = lambda a: pl.BlockSpec(a.shape, lambda i: (0,) * a.ndim)
    block = pl.BlockSpec((peers, 1, 2, row_count, bins), lambda i: (0, i, 0, 0, 0))
    row = pl.BlockSpec((1, 1, bins), lambda i: (i, 0, 0))
    return pl.pallas_call(
        body,
        grid=(own,),
        in_specs=[block, row, row, full(fh), full(fl), full(gh), full(gl), full(tc), full(ts)],
        out_specs=block,
        out_shape=jax.ShapeDtypeStruct(z.shape, BF),
        scratch_shapes=[
            pltpu.VMEM((outer, 2 * inner, 2 * bins), BF),
            pltpu.VMEM((outer, 2, inner, bins), F32),
        ],
        compiler_params=pltpu.CompilerParams(vmem_limit_bytes=VMEM_BYTES),
        name="channel_filter",
    )(z, limit, weight, fh, fl, gh, gl, tc, ts)


def time_inverse(h, th, tl, tc, ts, inner, rows):
    outer, _, row_count, half = h.shape
    samples = outer * inner
    tiles = inner // LANES
    sub = 8

    def body(h_ref, th_ref, tl_ref, tc_ref, ts_ref, o_ref, low_ref, g_ref):
        per = 8

        def product(g, carry):
            k0 = pl.multiple_of(g * per, per)
            hr = h_ref[pl.ds(k0, per), 0].reshape(per * rows, half)
            hi = h_ref[pl.ds(k0, per), 1].reshape(per * rows, half)
            hh = jnp.concatenate([hr, hi], axis=1)
            w = mm(hh, th_ref[...]) + mm(hh, tl_ref[...])
            g_ref[pl.ds(k0, per)] = w.reshape(per, rows, 2 * inner)
            return carry

        lax.fori_loop(0, outer // per, product, 0)

        def group(g, carry):
            r0 = pl.multiple_of(g * sub, sub)
            for t in range(tiles):
                lanes = slice(t * LANES, (t + 1) * LANES)
                ilanes = slice(inner + t * LANES, inner + (t + 1) * LANES)
                gs = []
                for k in range(outer):
                    wr = g_ref[k, pl.ds(r0, sub), lanes]
                    wi = g_ref[k, pl.ds(r0, sub), ilanes]
                    c = tc_ref[k : k + 1, lanes]
                    s = ts_ref[k : k + 1, lanes]
                    gs.append((wr * c - wi * s, wr * s + wi * c))
                hs = []
                for k in range(outer // 2 + 1):
                    a, b = gs[k], gs[(outer - k) % outer]
                    hs.append((a[0] + b[0], a[1] - b[1]))
                xs = c2r(hs, outer)
                for a in range(outer):
                    cols = slice(a * inner + t * LANES, a * inner + (t + 1) * LANES)
                    o_ref[pl.ds(r0, sub), cols] = xs[a]
            return carry

        lax.fori_loop(0, rows // sub, group, 0)
        low_ref[...] = o_ref[...].astype(BF)

    full = lambda a: pl.BlockSpec(a.shape, lambda i: (0,) * a.ndim)
    out_block = pl.BlockSpec((rows, samples), lambda i: (i, 0))
    return pl.pallas_call(
        body,
        grid=(row_count // rows,),
        in_specs=[pl.BlockSpec((outer, 2, rows, half), lambda i: (0, 0, i, 0)), full(th), full(tl), full(tc), full(ts)],
        out_specs=[out_block, out_block],
        out_shape=[
            jax.ShapeDtypeStruct((row_count, samples), F32),
            jax.ShapeDtypeStruct((row_count, samples), BF),
        ],
        scratch_shapes=[pltpu.VMEM((outer, rows, 2 * inner), F32)],
        compiler_params=pltpu.CompilerParams(vmem_limit_bytes=VMEM_BYTES),
        name="time_inverse",
    )(h, th, tl, tc, ts)


def window_energy(low, stack, step):
    depth, samples = low.shape
    width = stack.shape[1]
    windows = samples // WIN
    per_step = step // WIN
    chunk = 256

    def body(low_ref, st_ref, o_ref, e_ref):
        i = pl.program_id(0)
        lt = low_ref[...].T
        for n in range(width // chunk):
            cols = slice(n * chunk, (n + 1) * chunk)
            d = mm(lt, st_ref[:, cols])
            sq = d * d
            e_ref[pl.ds(pl.multiple_of(i * per_step, per_step), per_step), cols] = jnp.sum(
                sq.reshape(per_step, WIN, chunk), axis=1
            ) * (1.0 / WIN)

        @pl.when(i == pl.num_programs(0) - 1)
        def _():
            for n in range(width // chunk):
                cols = slice(n * chunk, (n + 1) * chunk)
                o_ref[cols, :] = e_ref[:, cols].T

    return pl.pallas_call(
        body,
        grid=(samples // step,),
        in_specs=[pl.BlockSpec((depth, step), lambda i: (0, i)), pl.BlockSpec(stack.shape, lambda i: (0, 0))],
        out_specs=pl.BlockSpec((width, windows), lambda i: (0, 0)),
        out_shape=jax.ShapeDtypeStruct((width, windows), F32),
        scratch_shapes=[pltpu.VMEM((windows, width), F32)],
        compiler_params=pltpu.CompilerParams(vmem_limit_bytes=VMEM_BYTES),
        name="window_energy",
    )(low, stack)


def toeplitz(kernel_low, depth, count):
    templates, span = kernel_low.shape
    u = jnp.pad(kernel_low, ((0, 0), (1, depth + 1 - 1 - span)))
    flat = jnp.tile(u, (1, count))[:, : count * depth]
    m = flat.reshape(templates, count, depth)
    return jnp.transpose(m, (2, 1, 0)).reshape(depth, count * templates)


def per_device(das_window, fan_bound, tap_offset, tap_weight):
    row_count, samples = das_window.shape
    devices = lax.axis_size("chan")
    channels = row_count * devices
    inner = 256
    outer = samples // inner
    half = inner // 2
    own = outer // devices
    chan_inner = 128
    chan_outer = channels // chan_inner
    assert outer % devices == 0 and row_count % chan_inner == 0

    t_fwd, t_inv, ttc, tts = time_tables(samples, inner)
    back_scale = 0.125
    tfh, tfl = np_split(t_fwd)
    tih, til = np_split(t_inv * (1.0 / (samples * back_scale)))
    ttc, tts = jnp.asarray(ttc), jnp.asarray(tts)
    c_fwd, c_inv, ctc, cts = chan_tables(channels, chan_inner)
    cfh, cfl = np_split(c_fwd)
    cgh, cgl = np_split(c_inv)

    spectrum = time_forward(das_window, jnp.asarray(tfh), jnp.asarray(tfl), ttc, tts, inner, 32)
    spectrum = spectrum.reshape(devices, own, 2, row_count, half)
    by_freq = lax.all_to_all(spectrum, "chan", split_axis=0, concat_axis=0, tiled=True)

    position = lax.axis_index("chan")
    by_outer = jnp.transpose(fan_bound.reshape(half, outer), (1, 0))
    limit = lax.dynamic_slice_in_dim(by_outer, position * own, own, 0).reshape(own, 1, half)
    bin_outer = lax.broadcasted_iota(jnp.int32, (own, 1, half), 0) + position * own
    bin_inner = lax.broadcasted_iota(jnp.int32, (own, 1, half), 2)
    scale = back_scale / channels
    weight = jnp.where(bin_outer + bin_inner == 0, 0.5 * scale, scale).astype(F32)
    ctw = jnp.broadcast_to(jnp.asarray(ctc)[:, :, None], (chan_outer, chan_inner, half))
    stw = jnp.broadcast_to(jnp.asarray(cts)[:, :, None], (chan_outer, chan_inner, half))
    back = channel_filter(
        by_freq, limit, weight, jnp.asarray(cfh), jnp.asarray(cfl), jnp.asarray(cgh), jnp.asarray(cgl), ctw, stw, chan_inner
    )
    by_channel = lax.all_to_all(back, "chan", split_axis=0, concat_axis=0, tiled=True)
    by_channel = by_channel.reshape(outer, 2, row_count, half)
    filtered, low = time_inverse(by_channel, jnp.asarray(tih), jnp.asarray(til), ttc, tts, inner, 32)

    up = [(i, i + 1) for i in range(devices - 1)]
    down = [(i + 1, i) for i in range(devices - 1)]
    before = lax.ppermute(low[row_count - EDGE :], "chan", up)
    after = lax.ppermute(low[:EDGE], "chan", down)

    offsets_grid = jnp.arange(2 * HALO + 1, dtype=jnp.int32) - HALO
    matches = (tap_offset[:, :, None] == offsets_grid[None, None, :]).astype(F32)
    kernel_low = jnp.sum(tap_weight[:, :, None] * matches, axis=1).astype(BF)
    templates = kernel_low.shape[0]
    inside = toeplitz(kernel_low, row_count, row_count - 2 * EDGE)
    edge = toeplitz(kernel_low, 3 * EDGE, EDGE)
    edges = jnp.concatenate(
        [jnp.pad(edge, ((0, 0), (0, edge.shape[1]))), jnp.pad(edge, ((0, 0), (edge.shape[1], 0)))], axis=0
    )
    e_in = window_energy(low, inside, 512)
    ends = jnp.concatenate([before, low[: 2 * EDGE], low[row_count - 2 * EDGE :], after], axis=0)
    e_out = window_energy(ends, edges, 512)
    windows = samples // WIN
    cut = EDGE * templates
    energy = jnp.concatenate([e_out[:cut], e_in, e_out[cut:]], axis=0)
    return filtered, energy.reshape(row_count, templates, windows)


def solution(mesh):
    return jax.shard_map(
        per_device,
        mesh=mesh,
        in_specs=(P(("survey", "chan"), None), P(), P(), P()),
        out_specs=(P(("survey", "chan"), None), P(("survey", "chan"), None, None)),
        check_vma=False,
    )
```
